32 devices in a mesh: ens: 2 (over y), space: 4 (over z), tm: 2 (over x), mom: 2 (over core).
Axes of the slice: x: 2, y: 2, z: 4, core: 2. Of those that a mesh axis runs over, the one named last changes fastest.
Arguments:
- eigvecs: bfloat16 [8, 2, 3, 256, 2048], P(('ens', 'tm'), None, None, None, 'space'), parts along dimension 0, may hold values from -0.359375 to 0.359375
- momenta: int32 [4, 3], P('mom'), may hold values from 1 to 2
- pairs: int32 [2, 2], replicated, may hold values from 0 to 3, as said below
- spin_weights: float32 [4, 4], replicated, may hold values from -1 to 1
- perambulators: bfloat16 [4, 2, 4, 4, 256, 256], P(('ens', 'tm'), None, None, None, 'space'), parts along dimension 0, may hold values from -0.0234375 to 0.0234375
Outputs:
- blocks: bfloat16 [4, 4, 2, 256, 256], P(('ens', 'tm'), 'mom', None, 'space'), parts along dimension 0
The draws below stay inside these ranges and needn't reach their ends.
There are 2 independent parts, one for each index of `ens`. The reference program is written for one: setup_inputs(seed, part) draws one part's arguments, and reference() takes and returns one part's arrays. A program takes and returns all parts, laid end to end along the dimension named above; an argument that names none is the same for every part. Nothing has to cross between parts.
Inputs may be any that keep to these rules, and one draw needn't show every extreme that they name: pairs[q, 0], the sink, lies in time group q: (q) * 2 <= pairs[q, 0] < (q + 1) * 2; pairs[q, 1], the source, is any timeslice.
All inputs are finite; a program needn't handle non-finite values.
Results may differ from the reference program's by a relative error of at most 0.008.
Values may be sent and summed in bfloat16 or wider, within the bound.
No kernel may reach another device: no remote copies, remote signals or barrier semaphores. Data moves between devices by JAX's collectives and lax.ppermute only.
A program may use at most 64 MiB of HBM per device.

```python
import math
import jax
import jax.numpy as jnp
from jax import lax

NV = 256
SPIN = 4
LAT = 48
T_DEV = 2
PAIR_DEV = 1
SITES = 2048
TIMES = 4
NMOM = 4
PAIRS = 2


def draw_pairs(key, part):
    base = jax.random.fold_in(key, 71)
    first_key, second_key = jax.random.split(base)
    owners = jnp.arange(PAIRS, dtype=jnp.int32) // PAIR_DEV
    sinks = owners * T_DEV + jax.random.randint(first_key, (PAIRS,), 0, T_DEV, dtype=jnp.int32)
    sources = jax.random.randint(second_key, (PAIRS,), 0, TIMES, dtype=jnp.int32)
    sources = sources.at[0].set(TIMES - 1)
    sources = sources.at[PAIRS - 1].set(0)
    return jnp.stack([sinks, sources], 1).astype(jnp.int32)


def touch_ends(drawn, key, low, top_value):
    extent = drawn.shape
    spot = [jax.random.randint(jax.random.fold_in(key, axis), (), 0, extent[axis]) for axis in range(len(extent))]
    drawn = drawn.at[tuple(spot)].set(low)
    longest = extent.index(max(extent))
    spot[longest] = (spot[longest] + 1) % extent[longest]
    return drawn.at[tuple(spot)].set(top_value)


def steps_of(rng, extent, pieces, smallest, largest):
    factor_of = 1.0
    for position, parts in pieces:
        heights = jax.random.uniform(jax.random.fold_in(jax.random.fold_in(rng, 6), position), (parts,), jnp.float32, smallest / len(pieces), largest / len(pieces))
        factor_of = factor_of * jnp.repeat(jnp.exp(heights), extent[position] // parts).reshape((-1,) + (1,) * (len(extent) - 1 - position))
    return factor_of


def scatter_about(stream_key, dims, width, bound, cuts=(), held_as=jnp.bfloat16):
    drawn = width * jax.random.normal(stream_key, dims, jnp.float32)
    if cuts:
        drawn = drawn * steps_of(stream_key, dims, cuts, -0.22, 0.18)
    return jnp.clip(drawn, -bound, bound).astype(held_as)


def setup_inputs(seed: int = 0, part: int = 0) -> dict:
    seeds = jax.random.split(jax.random.key(seed), 6)
    part_keys = jax.random.split(jax.random.fold_in(seeds[5], part), 6)
    eigvecs = scatter_about(part_keys[0], (TIMES, 2, 3, NV, SITES), 0.06, 0.359375, ((0, 2), (4, 4)))
    momenta = touch_ends(jax.random.randint(seeds[1], (NMOM, 3), 1, 3), jax.random.fold_in(seeds[1], 1), 1, 2).astype(jnp.int32)
    pairs = draw_pairs(jax.random.fold_in(seeds[5], 71), part)
    spin_weights = scatter_about(seeds[3], (SPIN, SPIN), 0.25, 1.0, (), jnp.float32)
    perambulators = scatter_about(part_keys[4], (PAIRS, 2, SPIN, SPIN, NV, NV), (NV * NV) ** -0.5, 0.0234375, ((0, 2), (4, 4)))
    return dict(eigvecs=eigvecs, momenta=momenta, pairs=pairs, spin_weights=spin_weights, perambulators=perambulators)


EXACT_PRECISION = lax.Precision.HIGHEST


def phases(momenta, site_ids):
    xcoord = (site_ids % LAT).astype(jnp.float32)
    ycoord = ((site_ids // LAT) % LAT).astype(jnp.float32)
    zcoord = (site_ids // (LAT * LAT)).astype(jnp.float32)
    mom_float = momenta.astype(jnp.float32)
    angles = (mom_float[:, 0:1] * xcoord + mom_float[:, 1:2] * ycoord + mom_float[:, 2:3] * zcoord) * (2.0 * math.pi / LAT)
    return jnp.cos(angles), jnp.sin(angles)


def contract(left_array, right_array):
    return jnp.einsum('cis,cjs->ij', left_array, right_array, precision=EXACT_PRECISION)


def elemental_table(eigvecs, cosine_rows, sine_rows):
    def one_time(vector):
        real_wide = vector[0].astype(jnp.float32)
        imag_wide = vector[1].astype(jnp.float32)

        def one_mom(phase_pair):
            cosine, sine = phase_pair
            real_turned = (cosine * real_wide + sine * imag_wide).astype(jnp.bfloat16)
            imag_turned = (cosine * imag_wide - sine * real_wide).astype(jnp.bfloat16)
            real_turned, imag_turned = lax.optimization_barrier((real_turned, imag_turned))
            real_turned = real_turned.astype(jnp.float32)
            imag_turned = imag_turned.astype(jnp.float32)
            real_part = contract(real_wide, real_turned) + contract(imag_wide, imag_turned)
            imag_part = contract(real_wide, imag_turned) - contract(imag_wide, real_turned)
            return jnp.stack([real_part, imag_part]).astype(jnp.bfloat16)

        return lax.map(one_mom, (cosine_rows, sine_rows))

    return lax.map(one_time, eigvecs)


def bridge(mixed_block, source):
    real_part = jnp.einsum('kl,mjl->mkj', mixed_block[0], source[:, 0], precision=EXACT_PRECISION) + jnp.einsum('kl,mjl->mkj', mixed_block[1], source[:, 1], precision=EXACT_PRECISION)
    imag_part = jnp.einsum('kl,mjl->mkj', mixed_block[1], source[:, 0], precision=EXACT_PRECISION) - jnp.einsum('kl,mjl->mkj', mixed_block[0], source[:, 1], precision=EXACT_PRECISION)
    return jnp.stack([real_part, imag_part], 1).astype(jnp.bfloat16)


def attach(sink_elem, bridged):
    real_part = jnp.einsum('mik,mkj->mij', sink_elem[:, 0], bridged[:, 0], precision=EXACT_PRECISION) - jnp.einsum('mik,mkj->mij', sink_elem[:, 1], bridged[:, 1], precision=EXACT_PRECISION)
    imag_part = jnp.einsum('mik,mkj->mij', sink_elem[:, 0], bridged[:, 1], precision=EXACT_PRECISION) + jnp.einsum('mik,mkj->mij', sink_elem[:, 1], bridged[:, 0], precision=EXACT_PRECISION)
    return jnp.stack([real_part, imag_part], 1).astype(jnp.bfloat16)


def reference(eigvecs, momenta, pairs, spin_weights, perambulators):
    site_ids = jnp.arange(SITES, dtype=jnp.int32)
    cosine_rows, sine_rows = phases(momenta, site_ids)
    elementals = elemental_table(eigvecs, cosine_rows, sine_rows)
    mixed_peramb = jnp.einsum('ab,qcabkl->qckl', spin_weights.astype(jnp.float32), perambulators.astype(jnp.float32), precision=EXACT_PRECISION).astype(jnp.bfloat16)

    def one_pair(pair_item):
        pair_ids, mixed_block = pair_item
        sink_elem = elementals[pair_ids[0]].astype(jnp.float32)
        source = elementals[pair_ids[1]].astype(jnp.float32)
        bridged = bridge(mixed_block.astype(jnp.float32), source).astype(jnp.float32)
        return attach(sink_elem, bridged)

    return lax.map(one_pair, (pairs, mixed_peramb))
```

```python
import math

import jax
import jax.numpy as jnp
from jax import lax
from jax.experimental import pallas as pl
from jax.experimental.pallas import tpu as pltpu
from jax.sharding import PartitionSpec as P

LAT = 48
NT = (((1,), (1,)), ((), ()))
NN = (((1,), (0,)), ((), ()))


def phases(momenta, site_ids):
    xcoord = (site_ids % LAT).astype(jnp.float32)
    ycoord = (site_ids // LAT % LAT).astype(jnp.float32)
    zcoord = (site_ids // (LAT * LAT)).astype(jnp.float32)
    mom_float = momenta.astype(jnp.float32)
    angles = (
        mom_float[:, 0:1] * xcoord + mom_float[:, 1:2] * ycoord + mom_float[:, 2:3] * zcoord
    ) * (2.0 * math.pi / LAT)
    return (jnp.cos(angles), jnp.sin(angles))


def mm(left, right, dims):
    return lax.dot_general(left, right, dims, preferred_element_type=jnp.float32)


def elemental_kernel(scal, cos_ref, sin_ref, eig_ref, own_ref, *rest):
    sends, acc = rest[:-1], rest[-1]
    moms, rows = own_ref.shape[0], own_ref.shape[2]
    vecs, sites = eig_ref.shape[1:]
    places = len(sends) + 1
    step = pl.program_id(0)

    @pl.when(step == 0)
    def _():
        acc[...] = jnp.zeros_like(acc)

    both = eig_ref[...].reshape(2 * vecs, sites)
    real_wide = eig_ref[0].astype(jnp.float32)
    imag_wide = eig_ref[1].astype(jnp.float32)
    for m in range(moms):
        cosine, sine = cos_ref[m : m + 1, :], sin_ref[m : m + 1, :]
        real_turned = (cosine * real_wide + sine * imag_wide).astype(jnp.bfloat16)
        imag_turned = (cosine * imag_wide - sine * real_wide).astype(jnp.bfloat16)
        by_real = mm(both, real_turned, NT)
        by_imag = mm(both, imag_turned, NT)
        acc[m, 0] += by_real[:vecs] + by_imag[vecs:]
        acc[m, 1] += by_imag[:vecs] - by_real[vecs:]

    @pl.when(step == pl.num_programs(0) - 1)
    def _():
        for d, out in enumerate((own_ref, *sends)):
            first = pl.multiple_of(lax.rem(scal[0] + d, places) * rows, rows)
            out[...] = acc[:, :, pl.ds(first, rows), :].astype(out.dtype)


def partial_elementals(eigvecs, cosine, sine, scal, places):
    _, _, colours, vecs, sites = eigvecs.shape
    moms = cosine.shape[0]
    block = (moms, 2, vecs // places, vecs)
    whole = lambda c, s: (0, 0, 0, 0)
    return pl.pallas_call(
        elemental_kernel,
        grid_spec=pltpu.PrefetchScalarGridSpec(
            num_scalar_prefetch=1,
            grid=(colours,),
            in_specs=[
                pl.BlockSpec((moms, sites), lambda c, s: (0, 0)),
                pl.BlockSpec((moms, sites), lambda c, s: (0, 0)),
                pl.BlockSpec((None, 2, None, vecs, sites), lambda c, s: (s[1], 0, c, 0, 0)),
            ],
            out_specs=[pl.BlockSpec(block, whole)] * places,
            scratch_shapes=[pltpu.VMEM((moms, 2, vecs, vecs), jnp.float32)],
        ),
        out_shape=[jax.ShapeDtypeStruct(block, jnp.float32)]
        + [jax.ShapeDtypeStruct(block, jnp.bfloat16)] * (places - 1),
        name="elementals",
    )(scal, cosine, sine, eigvecs)


def mix_kernel(scal, spin, per_ref, out_ref):
    pairs, _, sinks, sources = per_ref.shape[:4]
    for q in range(pairs):
        for c in range(2):
            total = None
            for a in range(sinks):
                for b in range(sources):
                    term = spin[a, b] * per_ref[q, c, a, b].astype(jnp.float32)
                    total = term if total is None else total + term
            out_ref[q, c] = total.astype(out_ref.dtype)


def mixed_rows(perambulators, spin_weights, scal, parts):
    pairs, _, sinks, sources, rows, vecs = perambulators.shape
    take = rows // parts
    return pl.pallas_call(
        mix_kernel,
        grid_spec=pltpu.PrefetchScalarGridSpec(
            num_scalar_prefetch=1,
            grid=(1,),
            in_specs=[
                pl.BlockSpec(memory_space=pltpu.SMEM),
                pl.BlockSpec(
                    (pairs, 2, sinks, sources, take, vecs), lambda i, s: (0, 0, 0, 0, s[2], 0)
                ),
            ],
            out_specs=pl.BlockSpec((pairs, 2, take, vecs), lambda i, s: (0, 0, 0, 0)),
        ),
        out_shape=jax.ShapeDtypeStruct((pairs, 2, take, vecs), jnp.bfloat16),
        name="mixing",
    )(scal, spin_weights, perambulators)


def product_kernel(places, parts, scal, sink_ref, *rest):
    sources, mixes = rest[:places], rest[places : 2 * places]
    out_ref, source, mixed = rest[2 * places :]
    pairs, moms, _, rows, vecs = sink_ref.shape
    take = rows // parts
    for q in range(pairs):
        for d in range(places):
            place = lax.rem(scal[0] + (places - d), places)
            first = pl.multiple_of(place * rows, rows)
            source[:, :, pl.ds(first, rows), :] = sources[d][q]
            for h in range(parts):
                start = pl.multiple_of(place * rows + h * take, take)
                mixed[:, pl.ds(start, take), :] = mixes[d][h, q]
        for m in range(moms):
            both = sink_ref[q, m].reshape(2 * rows, vecs)
            by_real = mm(both, mixed[0], NN)
            by_imag = mm(both, mixed[1], NN)
            left_real = (by_real[:rows] - by_imag[rows:]).astype(jnp.bfloat16)
            left_imag = (by_imag[:rows] + by_real[rows:]).astype(jnp.bfloat16)
            left = jnp.concatenate([left_real, left_imag], 0)
            on_real = mm(left, source[m, 0], NT)
            on_imag = mm(left, source[m, 1], NT)
            out_ref[q, m, 0] = (on_real[:rows] + on_imag[rows:]).astype(out_ref.dtype)
            out_ref[q, m, 1] = (on_real[rows:] - on_imag[:rows]).astype(out_ref.dtype)


def products(sink, sources, mixes, scal):
    places, parts = len(sources), mixes[0].shape[0]
    pairs, moms, _, rows, vecs = sink.shape
    vmem = pl.BlockSpec(memory_space=pltpu.VMEM)
    return pl.pallas_call(
        lambda *refs: product_kernel(places, parts, *refs),
        in_specs=[pl.BlockSpec(memory_space=pltpu.SMEM)] + [vmem] * (1 + 2 * places),
        out_specs=vmem,
        out_shape=jax.ShapeDtypeStruct(sink.shape, jnp.bfloat16),
        scratch_shapes=[
            pltpu.VMEM((moms, 2, vecs, vecs), jnp.bfloat16),
            pltpu.VMEM((2, vecs, vecs), jnp.bfloat16),
        ],
        name="products",
    )(scal, sink, *sources, *mixes)


def shifted(value, axis, size, by):
    return lax.ppermute(value, axis, [(i, (i + by) % size) for i in range(size)])


def pick(stack, index):
    chosen = stack[0]
    for k in range(1, len(stack)):
        chosen = jnp.where(index == k, stack[k], chosen)
    return chosen


def local(eigvecs, momenta, pairs, spin_weights, perambulators):
    times_dev, sites_dev = eigvecs.shape[0], eigvecs.shape[4]
    pair_dev, rows_dev = perambulators.shape[0], perambulators.shape[4]
    tm_size, space_size, mom_size = (lax.axis_size(n) for n in ("tm", "space", "mom"))
    my_group, my_place = lax.axis_index("tm"), lax.axis_index("space")
    site_ids = my_place * sites_dev + jnp.arange(sites_dev, dtype=jnp.int32)
    cosine, sine = phases(momenta, site_ids)
    parts = mom_size if rows_dev % (16 * mom_size) == 0 else 1

    asked = []
    for d in range(1, tm_size):
        for p in range(pair_dev):
            asked.append(pairs[(my_group + d) % tm_size * pair_dev + p, 1])
    first = jnp.int32(0)
    for time in reversed(asked):
        first = jnp.where(time // times_dev == my_group, time % times_dev, first)

    def slot_of(time):
        return (time % times_dev - first) % times_dev

    half = lax.axis_index("mom") if parts > 1 else jnp.int32(0)
    slots = []
    for k in range(times_dev):
        scal = jnp.stack([my_place, (first + k) % times_dev, half])
        own, *sends = partial_elementals(eigvecs, cosine, sine, scal, space_size)
        total = own
        for d, send in enumerate(sends, 1):
            total = total + shifted(send, "space", space_size, d).astype(jnp.float32)
        slots.append(total.astype(jnp.bfloat16))

    mine = mixed_rows(perambulators, spin_weights, scal, parts)
    mixes = [mine] + [shifted(mine, "space", space_size, d) for d in range(1, space_size)]
    if parts > 1:
        stacked = jnp.stack(mixes)
        held = [stacked] + [shifted(stacked, "mom", parts, d) for d in range(1, parts)]
        halves = [pick(held, (half - h) % parts) for h in range(parts)]
        mixes = [jnp.stack([value[d] for value in halves]) for d in range(space_size)]
    else:
        mixes = [value[None] for value in mixes]

    own_pairs = [pairs[my_group * pair_dev + p] for p in range(pair_dev)]
    few = (tm_size - 1) * pair_dev == 1
    source = jnp.stack([pick(slots, slot_of(pair[1])) for pair in own_pairs])
    for d in range(1, tm_size):
        wanted = asked[(d - 1) * pair_dev : d * pair_dev]
        out = jnp.stack([slots[0] if few else pick(slots, slot_of(time)) for time in wanted])
        arrived = shifted(out, "tm", tm_size, d)
        for p, pair in enumerate(own_pairs):
            here = pair[1] // times_dev == (my_group - d) % tm_size
            source = source.at[p].set(jnp.where(here, arrived[p], source[p]))
    sources = [source] + [shifted(source, "space", space_size, d) for d in range(1, space_size)]
    sink = jnp.stack([pick(slots, slot_of(pair[0])) for pair in own_pairs])
    return products(sink, sources, mixes, scal)


def solution(mesh):
    return jax.shard_map(
        local,
        mesh=mesh,
        in_specs=(
            P(("ens", "tm"), None, None, None, "space"),
            P("mom", None),
            P(),
            P(),
            P(("ens", "tm"), None, None, None, "space", None),
        ),
        out_specs=P(("ens", "tm"), "mom", None, "space", None),
        check_vma=False,
    )
```

```python
import math

import jax
import jax.numpy as jnp
from jax import lax
from jax.experimental import pallas as pl
from jax.experimental.pallas import tpu as pltpu
from jax.sharding import PartitionSpec as P

LAT = 48
DIRECT = 4
NT = (((1,), (1,)), ((), ()))
NN = (((1,), (0,)), ((), ()))
SMEM = pl.BlockSpec(memory_space=pltpu.SMEM)
VMEM = pl.BlockSpec(memory_space=pltpu.VMEM)
ANY = pl.BlockSpec(memory_space=pl.ANY)
HBM = pl.BlockSpec(memory_space=pltpu.HBM)
LARGE = pltpu.CompilerParams(vmem_limit_bytes=16 * 2**20)
SMALL = pltpu.CompilerParams(vmem_limit_bytes=8 * 2**20)


def mm(left, right, dims):
    return lax.dot_general(left, right, dims, preferred_element_type=jnp.float32)


def asked_times(pairs, tm_size, pair_dev):
    group = lax.axis_index("tm")
    return [
        pairs[lax.rem(group + d, tm_size) * pair_dev + p, 1]
        for d in range(1, tm_size)
        for p in range(pair_dev)
    ]


def first_time(asked, times_dev):
    group = lax.axis_index("tm")
    first = jnp.int32(0)
    for time in reversed(asked):
        first = jnp.where(lax.div(time, times_dev) == group, lax.rem(time, times_dev), first)
    return first


def slot_of(time, first, times_dev):
    return lax.rem(lax.rem(time, times_dev) - first + times_dev, times_dev)


def phases(momenta, moms, first_site, sites):
    site = first_site + lax.broadcasted_iota(jnp.int32, (1, sites), 1)
    xcoord = (site % LAT).astype(jnp.float32)
    ycoord = (site // LAT % LAT).astype(jnp.float32)
    zcoord = (site // (LAT * LAT)).astype(jnp.float32)
    found = []
    for m in range(moms):
        px, py, pz = (momenta[m, k].astype(jnp.float32) for k in range(3))
        angles = (px * xcoord + py * ycoord + pz * zcoord) * (2.0 * math.pi / LAT)
        found.append((jnp.cos(angles), jnp.sin(angles)))
    return found


def mix(spin, per, out):
    for q in range(per.shape[0]):
        for c in range(2):
            total = None
            for a in range(per.shape[2]):
                for b in range(per.shape[3]):
                    term = spin[a, b] * per[q, c, a, b].astype(jnp.float32)
                    total = term if total is None else total + term
            out[q, c] = total.astype(out.dtype)


def elemental_kernel(slot, tm_size, places, direct, parts, pair_dev, momenta, pairs, *refs):
    mixing = parts > 0
    n_outs = places if direct else 2
    if mixing:
        spin, eig, per, mixed, *refs = refs
    else:
        eig, *refs = refs
    outs, (held, acc, sems, *more) = refs[:n_outs], refs[n_outs:]
    times, _, colours, vecs, sites = eig.shape
    moms, rows = outs[0].shape[-4], outs[0].shape[-2]
    place = lax.axis_index("space")
    first = first_time(asked_times(pairs, tm_size, pair_dev), times)
    time = lax.rem(first + slot, times)
    copies = [
        pltpu.make_async_copy(eig.at[time, :, c], held.at[c], sems.at[c]) for c in range(colours)
    ]
    for copy in copies:
        copy.start()
    if mixing:
        per_held, per_sem = more
        take = per_held.shape[4]
        start = 0 if parts == 1 else pl.multiple_of(lax.axis_index("mom") * take, take)
        per_copy = pltpu.make_async_copy(
            per.at[:, :, :, :, pl.ds(start, take), :], per_held, per_sem
        )
        per_copy.start()
    turns = phases(momenta, moms, place * sites, sites)
    for c in range(colours):
        copies[c].wait()
        both = held[c].reshape(2 * vecs, sites)
        real_wide = held[c, 0].astype(jnp.float32)
        imag_wide = held[c, 1].astype(jnp.float32)
        for m, (cosine, sine) in enumerate(turns):
            real_turned = (cosine * real_wide + sine * imag_wide).astype(jnp.bfloat16)
            imag_turned = (cosine * imag_wide - sine * real_wide).astype(jnp.bfloat16)
            by_real = mm(both, real_turned, NT)
            by_imag = mm(both, imag_turned, NT)
            real_part = by_real[:vecs] + by_imag[vecs:]
            imag_part = by_imag[:vecs] - by_real[vecs:]
            if c == 0:
                acc[m, 0] = real_part
                acc[m, 1] = imag_part
            else:
                acc[m, 0] += real_part
                acc[m, 1] += imag_part
    if mixing:
        per_copy.wait()
        mix(spin, per_held, mixed)
    for d in range(places):
        out = outs[d] if direct else outs[d % 2].at[d // 2]
        row = pl.multiple_of((place ^ d) * rows, rows)
        out[...] = acc[:, :, pl.ds(row, rows), :].astype(out.dtype)


def partial_elementals(
    slot, momenta, pairs, eigvecs, tm_size, places, direct, pair_dev, mixing=None
):
    _, _, colours, vecs, sites = eigvecs.shape
    block = (momenta.shape[0], 2, vecs // places, vecs)
    if direct:
        shapes = [jax.ShapeDtypeStruct(block, jnp.float32)]
        shapes += [jax.ShapeDtypeStruct(block, jnp.bfloat16)] * (places - 1)
    else:
        shapes = [
            jax.ShapeDtypeStruct((places // 2, *block), dtype) for dtype in (jnp.float32, jnp.bfloat16)
        ]
    scratch = [
        pltpu.VMEM((colours, 2, vecs, sites), jnp.bfloat16),
        pltpu.VMEM((block[0], 2, vecs, vecs), jnp.float32),
        pltpu.SemaphoreType.DMA((colours,)),
    ]
    ins, operands, parts = [SMEM, SMEM, HBM], (momenta, pairs, eigvecs), 0
    if mixing is not None:
        spin_weights, perambulators, parts = mixing
        count, _, sinks, sources, rows, _ = perambulators.shape
        ins = [SMEM, SMEM, SMEM, HBM, HBM]
        operands = (momenta, pairs, spin_weights, eigvecs, perambulators)
        shapes.insert(0, jax.ShapeDtypeStruct((count, 2, rows // parts, vecs), jnp.bfloat16))
        scratch.append(
            pltpu.VMEM((count, 2, sinks, sources, rows // parts, vecs), jnp.bfloat16)
        )
        scratch.append(pltpu.SemaphoreType.DMA)
    return pl.pallas_call(
        lambda *refs: elemental_kernel(slot, tm_size, places, direct, parts, pair_dev, *refs),
        in_specs=ins,
        out_specs=[VMEM] * len(shapes),
        out_shape=shapes,
        scratch_shapes=scratch,
        compiler_params=LARGE if parts else None,
        name="elementals_mixing" if parts else "elementals",
    )(*operands)


def added(terms):
    total = terms[0][...]
    for term in terms[1:]:
        total = total + term[...].astype(jnp.float32)
    return total.astype(jnp.bfloat16)


def source_kernel(tm_size, times, pair_dev, n_slots, pairs, *refs):
    slots, arrived, out_ref = refs[:n_slots], refs[n_slots:-1], refs[-1]
    group = lax.axis_index("tm")
    first = first_time(asked_times(pairs, tm_size, pair_dev), times)
    for p in range(pair_dev):
        source = pairs[group * pair_dev + p, 1]
        owner, slot = lax.div(source, times), slot_of(source, first, times)
        for k in range(n_slots):
            here = slot == k if n_slots > 1 else True

            @pl.when((owner == group) & here)
            def _(k=k, p=p):
                out_ref[p] = slots[k][...]

        for d in range(1, tm_size):

            @pl.when(owner == lax.rem(group + tm_size - d, tm_size))
            def _(d=d, p=p):
                out_ref[p] = arrived[d - 1][p]


def choose_source(pairs, slots, arrived, tm_size, times, pair_dev):
    return pl.pallas_call(
        lambda *refs: source_kernel(tm_size, times, pair_dev, len(slots), *refs),
        in_specs=[SMEM] + [VMEM] * (len(slots) + len(arrived)),
        out_specs=VMEM,
        out_shape=jax.ShapeDtypeStruct((pair_dev, *slots[0].shape), jnp.bfloat16),
        compiler_params=SMALL,
        name="choose_source",
    )(pairs, *slots, *arrived)


def left_kernel(order, tm_size, times, n_mixes, pairs, *refs):
    mixes, ready = refs[:n_mixes], refs[n_mixes : n_mixes + times - 1]
    terms = refs[n_mixes + times - 1 : -3]
    out_ref, sink_ref, mixed = refs[-3:]
    pair_dev, moms, _, rows, vecs = out_ref.shape
    take = rows // n_mixes
    for e, pieces in enumerate(mixes):
        half = lax.rem(lax.axis_index("mom") + (n_mixes - e), n_mixes) if n_mixes > 1 else 0
        for n, d in enumerate(order):
            start = pl.multiple_of((lax.axis_index("space") ^ d) * rows + half * take, take)
            mixed[:, :, pl.ds(start, take), :] = pieces[n]
    first = first_time(asked_times(pairs, tm_size, pair_dev), times)
    for q in range(pair_dev):
        slot = slot_of(pairs[lax.axis_index("tm") * pair_dev + q, 0], first, times)
        sink_ref[...] = added(terms)
        for k in range(times - 1):

            @pl.when(slot == k)
            def _(k=k):
                sink_ref[...] = ready[k][...]

        for m in range(moms):
            both = sink_ref[m].reshape(2 * rows, vecs)
            by_real = mm(both, mixed[q, 0], NN)
            by_imag = mm(both, mixed[q, 1], NN)
            out_ref[q, m, 0] = (by_real[:rows] - by_imag[rows:]).astype(out_ref.dtype)
            out_ref[q, m, 1] = (by_imag[:rows] + by_real[rows:]).astype(out_ref.dtype)


def left_products(pairs, ready, terms, mixes, order, tm_size, pair_dev):
    block = terms[0].shape
    vecs = block[-1]
    return pl.pallas_call(
        lambda *refs: left_kernel(order, tm_size, len(ready) + 1, len(mixes), *refs),
        in_specs=[SMEM] + [VMEM] * (len(mixes) + len(ready) + len(terms)),
        out_specs=VMEM,
        out_shape=jax.ShapeDtypeStruct((pair_dev, *block), jnp.bfloat16),
        scratch_shapes=[
            pltpu.VMEM(block, jnp.bfloat16),
            pltpu.VMEM((pair_dev, 2, vecs, vecs), jnp.bfloat16),
        ],
        compiler_params=SMALL,
        name="left_products",
    )(pairs, *mixes, *ready, *terms)


def right_kernel(left_ref, *refs):
    sources, (out_ref, whole) = refs[:-2], refs[-2:]
    pairs, moms, _, rows, vecs = left_ref.shape
    for d, source in enumerate(sources):
        start = pl.multiple_of((lax.axis_index("space") ^ d) * rows, rows)
        whole[:, :, :, pl.ds(start, rows), :] = source[...]
    for q in range(pairs):
        for m in range(moms):
            left = left_ref[q, m].reshape(2 * rows, vecs)
            on_real = mm(left, whole[q, m, 0], NT)
            on_imag = mm(left, whole[q, m, 1], NT)
            out_ref[q, m, 0] = (on_real[:rows] + on_imag[rows:]).astype(out_ref.dtype)
            out_ref[q, m, 1] = (on_real[rows:] - on_imag[:rows]).astype(out_ref.dtype)


def right_products(left, sources):
    pairs, moms, _, _, vecs = left.shape
    return pl.pallas_call(
        right_kernel,
        in_specs=[VMEM] * (1 + len(sources)),
        out_specs=VMEM,
        out_shape=jax.ShapeDtypeStruct(left.shape, jnp.bfloat16),
        scratch_shapes=[pltpu.VMEM((pairs, moms, 2, vecs, vecs), jnp.bfloat16)],
        compiler_params=SMALL,
        name="right_products",
    )(left, *sources)


def swapped(value, places, by):
    return lax.ppermute(value, "space", [(i, i ^ by) for i in range(places)])


def shifted(value, axis, size, by):
    return lax.ppermute(value, axis, [(i, (i + by) % size) for i in range(size)])


def sum_of(terms):
    total = terms[0]
    for term in terms[1:]:
        total = total + term.astype(jnp.float32)
    return total.astype(jnp.bfloat16)


def pick(stack, index):
    chosen = stack[0]
    for k in range(1, len(stack)):
        chosen = jnp.where(index == k, stack[k], chosen)
    return chosen


def local(eigvecs, momenta, pairs, spin_weights, perambulators):
    times_dev = eigvecs.shape[0]
    pair_dev, rows_dev = perambulators.shape[0], perambulators.shape[4]
    tm_size, places, mom_size = (lax.axis_size(n) for n in ("tm", "space", "mom"))
    parts = mom_size if rows_dev % (16 * mom_size) == 0 else 1

    few = (tm_size - 1) * pair_dev == 1 and times_dev == 2
    owners = pairs[:, 1] // times_dev
    late = (owners[0] == owners[1]) & (pairs[0, 1] != pairs[1, 1])
    terms, late_pairs = [], pairs
    for k in range(times_dev):
        last = k == times_dev - 1
        direct = k == 0 and places <= DIRECT
        blocks = partial_elementals(
            k, momenta, late_pairs, eigvecs, tm_size, places, direct, pair_dev,
            (spin_weights, perambulators, parts) if last else None,
        )
        late_pairs, blocks = lax.optimization_barrier((pairs, blocks))
        if last:
            mine, *blocks = blocks
        if direct:
            own, *sends = blocks
            terms.append([own] + [swapped(s, places, d) for d, s in enumerate(sends, 1)])
        else:
            kept, sent = blocks
            by = 1
            received = swapped(sent, places, by)
            while kept.shape[0] > 1:
                total = kept + received.astype(jnp.float32)
                kept, sent, by = total[0::2], total[1::2].astype(jnp.bfloat16), by * 2
                received = swapped(sent, places, by)
            terms.append([kept[0], received[0]])
    ready = [sum_of(parts_of) for parts_of in terms[:-1]]

    mixes, order, by = mine[None], [0], places // 2
    while by:
        mixes = jnp.concatenate([mixes, swapped(mixes, places, by)])
        order += [d ^ by for d in order]
        by //= 2
    mixes = [mixes] + [shifted(mixes, "mom", parts, e) for e in range(1, parts)]

    def gather(source):
        there = {d: swapped(source, places, d) for d in sorted(range(1, places), key=lambda d: -(d ^ 1))}
        return [source] + [there[d] for d in range(1, places)]

    left = left_products(pairs, ready, terms[-1], mixes, order, tm_size, pair_dev)
    if few:
        arrived = [shifted(ready[0][None], "tm", tm_size, 1)]
        sources = gather(choose_source(pairs, ready, arrived, tm_size, times_dev, pair_dev))
        return lax.cond(
            late,
            lambda left, final, *sources: right_products(left, gather(late_source(pairs, sources[0], final, times_dev))),
            lambda left, final, *sources: right_products(left, sources),
            left, terms[-1], *sources,
        )
    asked = asked_times(pairs, tm_size, pair_dev)
    first = first_time(asked, times_dev)
    slots = ready + [sum_of(terms[-1])]
    out = [pick(slots, slot_of(time, first, times_dev)) for time in asked]
    arrived = [
        shifted(jnp.stack(out[(d - 1) * pair_dev : d * pair_dev]), "tm", tm_size, d)
        for d in range(1, tm_size)
    ]
    sources = gather(choose_source(pairs, slots, arrived, tm_size, times_dev, pair_dev))
    return right_products(left, sources)


def late_source(pairs, source, final, times_dev):
    mine = pairs[lax.axis_index("tm"), 1] // times_dev == lax.axis_index("tm")
    return jnp.where(mine, sum_of(final)[None], source)


def solution(mesh):
    return jax.shard_map(
        local,
        mesh=mesh,
        in_specs=(
            P(("ens", "tm"), None, None, None, "space"),
            P("mom", None),
            P(),
            P(),
            P(("ens", "tm"), None, None, None, "space", None),
        ),
        out_specs=P(("ens", "tm"), "mom", None, "space", None),
        check_vma=False,
    )
```

```python
import math

import jax
import jax.numpy as jnp
from jax import lax
from jax.experimental import pallas as pl
from jax.experimental.pallas import tpu as pltpu
from jax.sharding import PartitionSpec as P

LAT = 48
DIRECT = 4
NT = (((1,), (1,)), ((), ()))
NN = (((1,), (0,)), ((), ()))
SMEM = pl.BlockSpec(memory_space=pltpu.SMEM)
VMEM = pl.BlockSpec(memory_space=pltpu.VMEM)
ANY = pl.BlockSpec(memory_space=pl.ANY)
HBM = pl.BlockSpec(memory_space=pltpu.HBM)
LARGE = pltpu.CompilerParams(vmem_limit_bytes=16 * 2**20)
SMALL = pltpu.CompilerParams(vmem_limit_bytes=8 * 2**20)


def mm(left, right, dims):
    return lax.dot_general(left, right, dims, preferred_element_type=jnp.float32)


def asked_times(pairs, tm_size, pair_dev):
    group = lax.axis_index("tm")
    return [
        pairs[lax.rem(group + d, tm_size) * pair_dev + p, 1]
        for d in range(1, tm_size)
        for p in range(pair_dev)
    ]


def first_time(pairs, tm_size, pair_dev, times_dev):
    group = lax.axis_index("tm")
    asked = asked_times(pairs, tm_size, pair_dev)
    asked += [pairs[group * pair_dev + p, 1] for p in range(pair_dev)]
    first = jnp.int32(0)
    for time in reversed(asked):
        first = jnp.where(lax.div(time, times_dev) == group, lax.rem(time, times_dev), first)
    return first


def slot_of(time, first, times_dev):
    return lax.rem(lax.rem(time, times_dev) - first + times_dev, times_dev)


def whole_part(value, by):
    return jnp.floor((value + 0.5) * (1.0 / by))


def phases(momenta, moms, first_site, sites):
    shape = (2 * moms, sites)
    row = lax.broadcasted_iota(jnp.int32, shape, 0)
    site = (first_site + lax.broadcasted_iota(jnp.int32, shape, 1)).astype(jnp.float32)
    zcoord = whole_part(site, LAT * LAT)
    rest = site - zcoord * (LAT * LAT)
    ycoord = whole_part(rest, LAT)
    xcoord = rest - ycoord * LAT
    turns = jnp.where(row % 2 == 0, 0.0, 0.75 * LAT)
    for k, coord in enumerate((xcoord, ycoord, zcoord)):
        component = momenta[moms - 1, k].astype(jnp.float32)
        for m in reversed(range(moms - 1)):
            component = jnp.where(row < 2 * (m + 1), momenta[m, k].astype(jnp.float32), component)
        turns = turns + component * coord
    turns = turns - LAT * whole_part(turns, LAT)
    turns = jnp.where(turns < LAT / 2, turns, turns - LAT)
    rows = jnp.cos(turns * (2.0 * math.pi / LAT))
    return [(rows[2 * m : 2 * m + 1], rows[2 * m + 1 : 2 * m + 2]) for m in range(moms)]


def mix(spin, per, out):
    for q in range(per.shape[0]):
        for c in range(2):
            total = None
            for a in range(per.shape[2]):
                for b in range(per.shape[3]):
                    term = spin[a, b] * per[q, c, a, b].astype(jnp.float32)
                    total = term if total is None else total + term
            out[q, c] = total.astype(out.dtype)


def elemental_kernel(slot, tm_size, places, direct, parts, pair_dev, momenta_hbm, pairs_hbm, *refs):
    mixing = parts > 0
    n_outs = places if direct else 2
    if mixing:
        spin, eig, per, mixed, *refs = refs
    else:
        eig, *refs = refs
    outs, (early, held, acc, momenta, pairs, sems, small, *more) = refs[:n_outs], refs[n_outs:]
    times, _, colours, vecs, sites = eig.shape
    moms, rows = outs[0].shape[-4], outs[0].shape[-2]
    place = lax.axis_index("space")
    pairs_copy = pltpu.make_async_copy(pairs_hbm, pairs, small.at[0])
    momenta_copy = pltpu.make_async_copy(momenta_hbm, momenta, small.at[1])
    pairs_copy.start()
    momenta_copy.start()
    ahead = [
        pltpu.make_async_copy(eig.at[t, :, 0], early.at[t], sems.at[colours - 1 + t])
        for t in range(times)
    ]
    for copy in ahead:
        copy.start()
    pairs_copy.wait()
    first = first_time(pairs, tm_size, pair_dev, times)
    time = lax.rem(first + slot, times)
    copies = [
        pltpu.make_async_copy(eig.at[time, :, c], held.at[c - 1], sems.at[c - 1])
        for c in range(1, colours)
    ]
    for copy in copies:
        copy.start()
    if mixing:
        per_held, per_sem = more
        take = per_held.shape[4]
        start = 0 if parts == 1 else pl.multiple_of(lax.axis_index("mom") * take, take)
        per_copy = pltpu.make_async_copy(
            per.at[:, :, :, :, pl.ds(start, take), :], per_held, per_sem
        )
        per_copy.start()
    momenta_copy.wait()
    turns = phases(momenta, moms, place * sites, sites)
    for c in range(colours):
        if c == 0:
            for copy in ahead:
                copy.wait()
        else:
            copies[c - 1].wait()
        pair = early.at[time] if c == 0 else held.at[c - 1]
        both = pair[...].reshape(2 * vecs, sites)
        real_wide = pair[0].astype(jnp.float32)
        imag_wide = pair[1].astype(jnp.float32)
        for m, (cosine, sine) in enumerate(turns):
            real_turned = (cosine * real_wide + sine * imag_wide).astype(jnp.bfloat16)
            imag_turned = (cosine * imag_wide - sine * real_wide).astype(jnp.bfloat16)
            by_real = mm(both, real_turned, NT)
            by_imag = mm(both, imag_turned, NT)
            real_part = by_real[:vecs] + by_imag[vecs:]
            imag_part = by_imag[:vecs] - by_real[vecs:]
            if c == 0:
                acc[m, 0] = real_part
                acc[m, 1] = imag_part
            else:
                acc[m, 0] += real_part
                acc[m, 1] += imag_part
    if mixing:
        per_copy.wait()
        mix(spin, per_held, mixed)
    for d in range(places):
        out = outs[d] if direct else outs[d % 2].at[d // 2]
        row = pl.multiple_of((place ^ d) * rows, rows)
        out[...] = acc[:, :, pl.ds(row, rows), :].astype(out.dtype)


def partial_elementals(
    slot, momenta, pairs, eigvecs, tm_size, places, direct, pair_dev, mixing=None
):
    times, _, colours, vecs, sites = eigvecs.shape
    block = (momenta.shape[0], 2, vecs // places, vecs)
    if direct:
        shapes = [jax.ShapeDtypeStruct(block, jnp.float32)]
        shapes += [jax.ShapeDtypeStruct(block, jnp.bfloat16)] * (places - 1)
    else:
        shapes = [
            jax.ShapeDtypeStruct((places // 2, *block), dtype) for dtype in (jnp.float32, jnp.bfloat16)
        ]
    scratch = [
        pltpu.VMEM((times, 2, vecs, sites), jnp.bfloat16),
        pltpu.VMEM((colours - 1, 2, vecs, sites), jnp.bfloat16),
        pltpu.VMEM((block[0], 2, vecs, vecs), jnp.float32),
        pltpu.SMEM(momenta.shape, jnp.int32),
        pltpu.SMEM(pairs.shape, jnp.int32),
        pltpu.SemaphoreType.DMA((colours - 1 + times,)),
        pltpu.SemaphoreType.DMA((2,)),
    ]
    ins, operands, parts = [HBM, HBM, HBM], (momenta, pairs, eigvecs), 0
    if mixing is not None:
        spin_weights, perambulators, parts = mixing
        count, _, sinks, sources, rows, _ = perambulators.shape
        ins = [HBM, HBM, SMEM, HBM, HBM]
        operands = (momenta, pairs, spin_weights, eigvecs, perambulators)
        shapes.insert(0, jax.ShapeDtypeStruct((count, 2, rows // parts, vecs), jnp.bfloat16))
        scratch.append(
            pltpu.VMEM((count, 2, sinks, sources, rows // parts, vecs), jnp.bfloat16)
        )
        scratch.append(pltpu.SemaphoreType.DMA)
    return pl.pallas_call(
        lambda *refs: elemental_kernel(slot, tm_size, places, direct, parts, pair_dev, *refs),
        in_specs=ins,
        out_specs=[VMEM] * len(shapes),
        out_shape=shapes,
        scratch_shapes=scratch,
        compiler_params=LARGE if parts else None,
        name="elementals_mixing" if parts else "elementals",
    )(*operands)


def added(terms):
    total = terms[0][...]
    for term in terms[1:]:
        total = total + term[...].astype(jnp.float32)
    return total.astype(jnp.bfloat16)


def source_kernel(tm_size, times, pair_dev, n_slots, pairs, *refs):
    slots, arrived, out_ref = refs[:n_slots], refs[n_slots:-1], refs[-1]
    group = lax.axis_index("tm")
    first = first_time(pairs, tm_size, pair_dev, times)
    for p in range(pair_dev):
        source = pairs[group * pair_dev + p, 1]
        owner, slot = lax.div(source, times), slot_of(source, first, times)
        for k in range(n_slots):
            here = slot == k if n_slots > 1 else True

            @pl.when((owner == group) & here)
            def _(k=k, p=p):
                out_ref[p] = slots[k][...]

        for d in range(1, tm_size):

            @pl.when(owner == lax.rem(group + tm_size - d, tm_size))
            def _(d=d, p=p):
                out_ref[p] = arrived[d - 1][p]


def choose_source(pairs, slots, arrived, tm_size, times, pair_dev):
    return pl.pallas_call(
        lambda *refs: source_kernel(tm_size, times, pair_dev, len(slots), *refs),
        in_specs=[SMEM] + [VMEM] * (len(slots) + len(arrived)),
        out_specs=VMEM,
        out_shape=jax.ShapeDtypeStruct((pair_dev, *slots[0].shape), jnp.bfloat16),
        compiler_params=SMALL,
        name="choose_source",
    )(pairs, *slots, *arrived)


def left_kernel(order, tm_size, times, n_mixes, pairs, *refs):
    mixes, ready = refs[:n_mixes], refs[n_mixes : n_mixes + times - 1]
    terms = refs[n_mixes + times - 1 : -3]
    out_ref, sink_ref, mixed = refs[-3:]
    pair_dev, moms, _, rows, vecs = out_ref.shape
    take = rows // n_mixes
    for e, pieces in enumerate(mixes):
        half = lax.rem(lax.axis_index("mom") + (n_mixes - e), n_mixes) if n_mixes > 1 else 0
        for n, d in enumerate(order):
            start = pl.multiple_of((lax.axis_index("space") ^ d) * rows + half * take, take)
            mixed[:, :, pl.ds(start, take), :] = pieces[n]
    first = first_time(pairs, tm_size, pair_dev, times)
    for q in range(pair_dev):
        slot = slot_of(pairs[lax.axis_index("tm") * pair_dev + q, 0], first, times)
        sink_ref[...] = added(terms)
        for k in range(times - 1):

            @pl.when(slot == k)
            def _(k=k):
                sink_ref[...] = ready[k][...]

        for m in range(moms):
            both = sink_ref[m].reshape(2 * rows, vecs)
            by_real = mm(both, mixed[q, 0], NN)
            by_imag = mm(both, mixed[q, 1], NN)
            out_ref[q, m, 0] = (by_real[:rows] - by_imag[rows:]).astype(out_ref.dtype)
            out_ref[q, m, 1] = (by_imag[:rows] + by_real[rows:]).astype(out_ref.dtype)


def left_products(pairs, ready, terms, mixes, order, tm_size, pair_dev):
    block = terms[0].shape
    vecs = block[-1]
    return pl.pallas_call(
        lambda *refs: left_kernel(order, tm_size, len(ready) + 1, len(mixes), *refs),
        in_specs=[SMEM] + [VMEM] * (len(mixes) + len(ready) + len(terms)),
        out_specs=VMEM,
        out_shape=jax.ShapeDtypeStruct((pair_dev, *block), jnp.bfloat16),
        scratch_shapes=[
            pltpu.VMEM(block, jnp.bfloat16),
            pltpu.VMEM((pair_dev, 2, vecs, vecs), jnp.bfloat16),
        ],
        compiler_params=SMALL,
        name="left_products",
    )(pairs, *mixes, *ready, *terms)


def right_kernel(left_ref, *refs):
    sources, (out_ref, whole) = refs[:-2], refs[-2:]
    pairs, moms, _, rows, vecs = left_ref.shape
    for d, source in enumerate(sources):
        start = pl.multiple_of((lax.axis_index("space") ^ d) * rows, rows)
        whole[:, :, :, pl.ds(start, rows), :] = source[...]
    for q in range(pairs):
        for m in range(moms):
            left = left_ref[q, m].reshape(2 * rows, vecs)
            on_real = mm(left, whole[q, m, 0], NT)
            on_imag = mm(left, whole[q, m, 1], NT)
            out_ref[q, m, 0] = (on_real[:rows] + on_imag[rows:]).astype(out_ref.dtype)
            out_ref[q, m, 1] = (on_real[rows:] - on_imag[:rows]).astype(out_ref.dtype)


def right_products(left, sources):
    pairs, moms, _, _, vecs = left.shape
    return pl.pallas_call(
        right_kernel,
        in_specs=[VMEM] * (1 + len(sources)),
        out_specs=VMEM,
        out_shape=jax.ShapeDtypeStruct(left.shape, jnp.bfloat16),
        scratch_shapes=[pltpu.VMEM((pairs, moms, 2, vecs, vecs), jnp.bfloat16)],
        compiler_params=SMALL,
        name="right_products",
    )(left, *sources)


def swapped(value, places, by):
    return lax.ppermute(value, "space", [(i, i ^ by) for i in range(places)])


def shifted(value, axis, size, by):
    return lax.ppermute(value, axis, [(i, (i + by) % size) for i in range(size)])


def sum_of(terms):
    total = terms[0]
    for term in terms[1:]:
        total = total + term.astype(jnp.float32)
    return total.astype(jnp.bfloat16)


def pick(stack, index):
    chosen = stack[0]
    for k in range(1, len(stack)):
        chosen = jnp.where(index == k, stack[k], chosen)
    return chosen


def local(eigvecs, momenta, pairs, spin_weights, perambulators):
    times_dev = eigvecs.shape[0]
    pair_dev, rows_dev = perambulators.shape[0], perambulators.shape[4]
    tm_size, places, mom_size = (lax.axis_size(n) for n in ("tm", "space", "mom"))
    parts = mom_size if rows_dev % (16 * mom_size) == 0 else 1

    few = (tm_size - 1) * pair_dev == 1 and times_dev == 2
    owners = pairs[:, 1] // times_dev
    late = (owners[0] == owners[1]) & (pairs[0, 1] != pairs[1, 1])
    terms, inputs = [], (momenta, pairs, spin_weights, eigvecs, perambulators)
    for k in range(times_dev):
        last = k == times_dev - 1
        direct = k == 0 and places <= DIRECT
        momenta, late_pairs, spin_weights, eigvecs, perambulators = inputs
        blocks = partial_elementals(
            k, momenta, late_pairs, eigvecs, tm_size, places, direct, pair_dev,
            (spin_weights, perambulators, parts) if last else None,
        )
        inputs, blocks = lax.optimization_barrier((inputs, blocks))
        if last:
            mine, *blocks = blocks
        if direct:
            own, *sends = blocks
            terms.append([own] + [swapped(s, places, d) for d, s in enumerate(sends, 1)])
        else:
            kept, sent = blocks
            by = 1
            received = swapped(sent, places, by)
            while kept.shape[0] > 1:
                total = kept + received.astype(jnp.float32)
                kept, sent, by = total[0::2], total[1::2].astype(jnp.bfloat16), by * 2
                received = swapped(sent, places, by)
            terms.append([kept[0], received[0]])
    ready = [sum_of(parts_of) for parts_of in terms[:-1]]

    mixes, order, by = mine[None], [0], places // 2
    while by:
        mixes = jnp.concatenate([mixes, swapped(mixes, places, by)])
        order += [d ^ by for d in order]
        by //= 2
    mixes = [mixes] + [shifted(mixes, "mom", parts, e) for e in range(1, parts)]

    def gather(source):
        there = {d: swapped(source, places, d) for d in sorted(range(1, places), key=lambda d: -(d ^ 1))}
        return [source] + [there[d] for d in range(1, places)]

    left = left_products(pairs, ready, terms[-1], mixes, order, tm_size, pair_dev)
    if few:
        arrived = [shifted(ready[0][None], "tm", tm_size, 1)]
        sources = gather(choose_source(pairs, ready, arrived, tm_size, times_dev, pair_dev))
        return lax.cond(
            late,
            lambda left, final, *sources: right_products(left, gather(late_source(pairs, sources[0], final, times_dev))),
            lambda left, final, *sources: right_products(left, sources),
            left, terms[-1], *sources,
        )
    asked = asked_times(pairs, tm_size, pair_dev)
    first = first_time(pairs, tm_size, pair_dev, times_dev)
    slots = ready + [sum_of(terms[-1])]
    out = [pick(slots, slot_of(time, first, times_dev)) for time in asked]
    arrived = [
        shifted(jnp.stack(out[(d - 1) * pair_dev : d * pair_dev]), "tm", tm_size, d)
        for d in range(1, tm_size)
    ]
    sources = gather(choose_source(pairs, slots, arrived, tm_size, times_dev, pair_dev))
    return right_products(left, sources)


def late_source(pairs, source, final, times_dev):
    mine = pairs[lax.axis_index("tm"), 1] // times_dev == lax.axis_index("tm")
    return jnp.where(mine, sum_of(final)[None], source)


def solution(mesh):
    return jax.shard_map(
        local,
        mesh=mesh,
        in_specs=(
            P(("ens", "tm"), None, None, None, "space"),
            P("mom", None),
            P(),
            P(),
            P(("ens", "tm"), None, None, None, "space", None),
        ),
        out_specs=P(("ens", "tm"), "mom", None, "space", None),
        check_vma=False,
    )
```

```python
import math

import jax
import jax.numpy as jnp
from jax import lax
from jax.experimental import pallas as pl
from jax.experimental.pallas import tpu as pltpu
from jax.sharding import PartitionSpec as P

LAT = 48
DIRECT = 0
NT = (((1,), (1,)), ((), ()))
NN = (((1,), (0,)), ((), ()))
SMEM = pl.BlockSpec(memory_space=pltpu.SMEM)
VMEM = pl.BlockSpec(memory_space=pltpu.VMEM)
ANY = pl.BlockSpec(memory_space=pl.ANY)
HBM = pl.BlockSpec(memory_space=pltpu.HBM)
LARGE = pltpu.CompilerParams(vmem_limit_bytes=16 * 2**20)
SMALL = pltpu.CompilerParams(vmem_limit_bytes=8 * 2**20)


def mm(left, right, dims):
    return lax.dot_general(left, right, dims, preferred_element_type=jnp.float32)


def asked_times(pairs, tm_size, pair_dev):
    group = lax.axis_index("tm")
    return [
        pairs[lax.rem(group + d, tm_size) * pair_dev + p, 1]
        for d in range(1, tm_size)
        for p in range(pair_dev)
    ]


def first_time(pairs, tm_size, pair_dev, times_dev):
    group = lax.axis_index("tm")
    asked = asked_times(pairs, tm_size, pair_dev)
    asked += [pairs[group * pair_dev + p, 1] for p in range(pair_dev)]
    first = jnp.int32(0)
    for time in reversed(asked):
        first = jnp.where(lax.div(time, times_dev) == group, lax.rem(time, times_dev), first)
    return first


def slot_of(time, first, times_dev):
    return lax.rem(lax.rem(time, times_dev) - first + times_dev, times_dev)


def whole_part(value, by):
    return jnp.floor((value + 0.5) * (1.0 / by))


def phases(momenta, moms, first_site, sites):
    shape = (2 * moms, sites)
    row = lax.broadcasted_iota(jnp.int32, shape, 0)
    site = (first_site + lax.broadcasted_iota(jnp.int32, shape, 1)).astype(jnp.float32)
    zcoord = whole_part(site, LAT * LAT)
    rest = site - zcoord * (LAT * LAT)
    ycoord = whole_part(rest, LAT)
    xcoord = rest - ycoord * LAT
    turns = jnp.where(row % 2 == 0, 0.0, 0.75 * LAT)
    for k, coord in enumerate((xcoord, ycoord, zcoord)):
        component = momenta[moms - 1, k].astype(jnp.float32)
        for m in reversed(range(moms - 1)):
            component = jnp.where(row < 2 * (m + 1), momenta[m, k].astype(jnp.float32), component)
        turns = turns + component * coord
    turns = turns - LAT * whole_part(turns, LAT)
    turns = jnp.where(turns < LAT / 2, turns, turns - LAT)
    rows = jnp.cos(turns * (2.0 * math.pi / LAT))
    return [(rows[2 * m : 2 * m + 1], rows[2 * m + 1 : 2 * m + 2]) for m in range(moms)]


def mix(spin, per, out):
    for q in range(per.shape[0]):
        for c in range(2):
            total = None
            for a in range(per.shape[2]):
                for b in range(per.shape[3]):
                    term = spin[a, b] * per[q, c, a, b].astype(jnp.float32)
                    total = term if total is None else total + term
            out[q, c] = total.astype(out.dtype)


def elemental_kernel(slot, tm_size, places, direct, parts, pair_dev, momenta_hbm, pairs_hbm, *refs):
    mixing = parts > 0
    n_outs = places if direct else 2
    if mixing:
        spin, eig, per, mixed, *refs = refs
    else:
        eig, *refs = refs
    outs, (early, held, acc, momenta, pairs, sems, small, *more) = refs[:n_outs], refs[n_outs:]
    times, _, colours, vecs, sites = eig.shape
    moms, rows = outs[0].shape[-4], outs[0].shape[-2]
    place = lax.axis_index("space")
    pairs_copy = pltpu.make_async_copy(pairs_hbm, pairs, small.at[0])
    momenta_copy = pltpu.make_async_copy(momenta_hbm, momenta, small.at[1])
    pairs_copy.start()
    momenta_copy.start()
    ahead = [
        pltpu.make_async_copy(eig.at[t, :, 0], early.at[t], sems.at[colours - 1 + t])
        for t in range(times)
    ]
    for copy in ahead:
        copy.start()
    pairs_copy.wait()
    first = first_time(pairs, tm_size, pair_dev, times)
    time = lax.rem(first + slot, times)
    copies = [
        pltpu.make_async_copy(eig.at[time, :, c], held.at[c - 1], sems.at[c - 1])
        for c in range(1, colours)
    ]
    for copy in copies:
        copy.start()
    if mixing:
        per_held, per_sem = more
        take = per_held.shape[4]
        start = 0 if parts == 1 else pl.multiple_of(lax.axis_index("mom") * take, take)
        per_copy = pltpu.make_async_copy(
            per.at[:, :, :, :, pl.ds(start, take), :], per_held, per_sem
        )
        per_copy.start()
    momenta_copy.wait()
    turns = phases(momenta, moms, place * sites, sites)
    for c in range(colours):
        if c == 0:
            for copy in ahead:
                copy.wait()
        else:
            copies[c - 1].wait()
        pair = early.at[time] if c == 0 else held.at[c - 1]
        both = pair[...].reshape(2 * vecs, sites)
        real_wide = pair[0].astype(jnp.float32)
        imag_wide = pair[1].astype(jnp.float32)
        for m, (cosine, sine) in enumerate(turns):
            real_turned = (cosine * real_wide + sine * imag_wide).astype(jnp.bfloat16)
            imag_turned = (cosine * imag_wide - sine * real_wide).astype(jnp.bfloat16)
            by_real = mm(both, real_turned, NT)
            by_imag = mm(both, imag_turned, NT)
            real_part = by_real[:vecs] + by_imag[vecs:]
            imag_part = by_imag[:vecs] - by_real[vecs:]
            if c == 0:
                acc[m, 0] = real_part
                acc[m, 1] = imag_part
            else:
                acc[m, 0] += real_part
                acc[m, 1] += imag_part
    if mixing:
        per_copy.wait()
        mix(spin, per_held, mixed)
    for d in range(places):
        out = outs[d] if direct else outs[d % 2].at[d // 2]
        row = pl.multiple_of((place ^ d) * rows, rows)
        out[...] = acc[:, :, pl.ds(row, rows), :].astype(out.dtype)


def partial_elementals(
    slot, momenta, pairs, eigvecs, tm_size, places, direct, pair_dev, mixing=None
):
    times, _, colours, vecs, sites = eigvecs.shape
    block = (momenta.shape[0], 2, vecs // places, vecs)
    if direct:
        shapes = [jax.ShapeDtypeStruct(block, jnp.float32)]
        shapes += [jax.ShapeDtypeStruct(block, jnp.bfloat16)] * (places - 1)
    else:
        shapes = [
            jax.ShapeDtypeStruct((places // 2, *block), dtype) for dtype in (jnp.float32, jnp.bfloat16)
        ]
    scratch = [
        pltpu.VMEM((times, 2, vecs, sites), jnp.bfloat16),
        pltpu.VMEM((colours - 1, 2, vecs, sites), jnp.bfloat16),
        pltpu.VMEM((block[0], 2, vecs, vecs), jnp.float32),
        pltpu.SMEM(momenta.shape, jnp.int32),
        pltpu.SMEM(pairs.shape, jnp.int32),
        pltpu.SemaphoreType.DMA((colours - 1 + times,)),
        pltpu.SemaphoreType.DMA((2,)),
    ]
    ins, operands, parts = [HBM, HBM, HBM], (momenta, pairs, eigvecs), 0
    if mixing is not None:
        spin_weights, perambulators, parts = mixing
        count, _, sinks, sources, rows, _ = perambulators.shape
        ins = [HBM, HBM, SMEM, HBM, HBM]
        operands = (momenta, pairs, spin_weights, eigvecs, perambulators)
        shapes.insert(0, jax.ShapeDtypeStruct((count, 2, rows // parts, vecs), jnp.bfloat16))
        scratch.append(
            pltpu.VMEM((count, 2, sinks, sources, rows // parts, vecs), jnp.bfloat16)
        )
        scratch.append(pltpu.SemaphoreType.DMA)
    return pl.pallas_call(
        lambda *refs: elemental_kernel(slot, tm_size, places, direct, parts, pair_dev, *refs),
        in_specs=ins,
        out_specs=[VMEM] * len(shapes),
        out_shape=shapes,
        scratch_shapes=scratch,
        compiler_params=LARGE if slot else None,
        name="elementals_mixing" if parts else "elementals",
    )(*operands)


def added(terms):
    total = terms[0][...]
    for term in terms[1:]:
        total = total + term[...].astype(jnp.float32)
    return total.astype(jnp.bfloat16)


def source_kernel(tm_size, times, pair_dev, n_slots, pairs, *refs):
    slots, arrived, out_ref = refs[:n_slots], refs[n_slots:-1], refs[-1]
    group = lax.axis_index("tm")
    first = first_time(pairs, tm_size, pair_dev, times)
    for p in range(pair_dev):
        source = pairs[group * pair_dev + p, 1]
        owner, slot = lax.div(source, times), slot_of(source, first, times)
        for k in range(n_slots):
            here = slot == k if n_slots > 1 else True

            @pl.when((owner == group) & here)
            def _(k=k, p=p):
                out_ref[p] = slots[k][...]

        for d in range(1, tm_size):

            @pl.when(owner == lax.rem(group + tm_size - d, tm_size))
            def _(d=d, p=p):
                out_ref[p] = arrived[d - 1][p]


def choose_source(pairs, slots, arrived, tm_size, times, pair_dev):
    return pl.pallas_call(
        lambda *refs: source_kernel(tm_size, times, pair_dev, len(slots), *refs),
        in_specs=[SMEM] + [VMEM] * (len(slots) + len(arrived)),
        out_specs=VMEM,
        out_shape=jax.ShapeDtypeStruct((pair_dev, *slots[0].shape), jnp.bfloat16),
        compiler_params=SMALL,
        name="choose_source",
    )(pairs, *slots, *arrived)


def left_kernel(order, tm_size, times, n_mixes, pairs, *refs):
    mixes, ready = refs[:n_mixes], refs[n_mixes : n_mixes + times - 1]
    terms = refs[n_mixes + times - 1 : -3]
    out_ref, sink_ref, mixed = refs[-3:]
    pair_dev, moms, _, rows, vecs = out_ref.shape
    take = rows // n_mixes
    for e, pieces in enumerate(mixes):
        half = lax.rem(lax.axis_index("mom") + (n_mixes - e), n_mixes) if n_mixes > 1 else 0
        for n, d in enumerate(order):
            start = pl.multiple_of((lax.axis_index("space") ^ d) * rows + half * take, take)
            mixed[:, :, pl.ds(start, take), :] = pieces[n]
    first = first_time(pairs, tm_size, pair_dev, times)
    for q in range(pair_dev):
        slot = slot_of(pairs[lax.axis_index("tm") * pair_dev + q, 0], first, times)
        sink_ref[...] = added(terms)
        for k in range(times - 1):

            @pl.when(slot == k)
            def _(k=k):
                sink_ref[...] = ready[k][...]

        for m in range(moms):
            both = sink_ref[m].reshape(2 * rows, vecs)
            by_real = mm(both, mixed[q, 0], NN)
            by_imag = mm(both, mixed[q, 1], NN)
            out_ref[q, m, 0] = (by_real[:rows] - by_imag[rows:]).astype(out_ref.dtype)
            out_ref[q, m, 1] = (by_imag[:rows] + by_real[rows:]).astype(out_ref.dtype)


def left_products(pairs, ready, terms, mixes, order, tm_size, pair_dev):
    block = terms[0].shape
    vecs = block[-1]
    return pl.pallas_call(
        lambda *refs: left_kernel(order, tm_size, len(ready) + 1, len(mixes), *refs),
        in_specs=[SMEM] + [VMEM] * (len(mixes) + len(ready) + len(terms)),
        out_specs=VMEM,
        out_shape=jax.ShapeDtypeStruct((pair_dev, *block), jnp.bfloat16),
        scratch_shapes=[
            pltpu.VMEM(block, jnp.bfloat16),
            pltpu.VMEM((pair_dev, 2, vecs, vecs), jnp.bfloat16),
        ],
        compiler_params=SMALL,
        name="left_products",
    )(pairs, *mixes, *ready, *terms)


def right_kernel(left_ref, *refs):
    sources, (out_ref, whole) = refs[:-2], refs[-2:]
    pairs, moms, _, rows, vecs = left_ref.shape
    for d, source in enumerate(sources):
        start = pl.multiple_of((lax.axis_index("space") ^ d) * rows, rows)
        whole[:, :, :, pl.ds(start, rows), :] = source[...]
    for q in range(pairs):
        for m in range(moms):
            left = left_ref[q, m].reshape(2 * rows, vecs)
            on_real = mm(left, whole[q, m, 0], NT)
            on_imag = mm(left, whole[q, m, 1], NT)
            out_ref[q, m, 0] = (on_real[:rows] + on_imag[rows:]).astype(out_ref.dtype)
            out_ref[q, m, 1] = (on_real[rows:] - on_imag[:rows]).astype(out_ref.dtype)


def right_products(left, sources):
    pairs, moms, _, _, vecs = left.shape
    return pl.pallas_call(
        right_kernel,
        in_specs=[VMEM] * (1 + len(sources)),
        out_specs=VMEM,
        out_shape=jax.ShapeDtypeStruct(left.shape, jnp.bfloat16),
        scratch_shapes=[pltpu.VMEM((pairs, moms, 2, vecs, vecs), jnp.bfloat16)],
        compiler_params=SMALL,
        name="right_products",
    )(left, *sources)


def swapped(value, places, by):
    return lax.ppermute(value, "space", [(i, i ^ by) for i in range(places)])


def shifted(value, axis, size, by):
    return lax.ppermute(value, axis, [(i, (i + by) % size) for i in range(size)])


def sum_of(terms):
    total = terms[0]
    for term in terms[1:]:
        total = total + term.astype(jnp.float32)
    return total.astype(jnp.bfloat16)


def pick(stack, index):
    chosen = stack[0]
    for k in range(1, len(stack)):
        chosen = jnp.where(index == k, stack[k], chosen)
    return chosen


def local(eigvecs, momenta, pairs, spin_weights, perambulators):
    times_dev = eigvecs.shape[0]
    pair_dev, rows_dev = perambulators.shape[0], perambulators.shape[4]
    tm_size, places, mom_size = (lax.axis_size(n) for n in ("tm", "space", "mom"))
    parts = mom_size if rows_dev % (16 * mom_size) == 0 else 1

    few = (tm_size - 1) * pair_dev == 1 and times_dev == 2
    owners = pairs[:, 1] // times_dev
    late = (owners[0] == owners[1]) & (pairs[0, 1] != pairs[1, 1])
    terms, inputs = [], (momenta, pairs, spin_weights, eigvecs, perambulators)
    for k in range(times_dev):
        direct = k == 0 and places <= DIRECT
        momenta, late_pairs, spin_weights, eigvecs, perambulators = inputs
        blocks = partial_elementals(
            k, momenta, late_pairs, eigvecs, tm_size, places, direct, pair_dev,
            (spin_weights, perambulators, parts) if k == times_dev - 1 else None,
        )
        inputs, blocks = lax.optimization_barrier((inputs, blocks))
        if k == times_dev - 1:
            mine, *blocks = blocks
        if direct:
            own, *sends = blocks
            terms.append([own] + [swapped(s, places, d) for d, s in enumerate(sends, 1)])
        else:
            kept, sent = blocks
            by = 1
            received = swapped(sent, places, by)
            while kept.shape[0] > 1:
                total = kept + received.astype(jnp.float32)
                kept, sent, by = total[0::2], total[1::2].astype(jnp.bfloat16), by * 2
                received = swapped(sent, places, by)
            terms.append([kept[0], received[0]])
    ready = [sum_of(parts_of) for parts_of in terms[:-1]]

    mixes, order, by = mine[None], [0], places // 2
    while by:
        mixes = jnp.concatenate([mixes, swapped(mixes, places, by)])
        order += [d ^ by for d in order]
        by //= 2
    mixes = [mixes] + [shifted(mixes, "mom", parts, e) for e in range(1, parts)]

    def gather(source):
        there = {d: swapped(source, places, d) for d in sorted(range(1, places), key=lambda d: -(d ^ 1))}
        return [source] + [there[d] for d in range(1, places)]

    left = left_products(pairs, ready, terms[-1], mixes, order, tm_size, pair_dev)
    if few:
        arrived = [shifted(ready[0][None], "tm", tm_size, 1)]
        sources = gather(choose_source(pairs, ready, arrived, tm_size, times_dev, pair_dev))
        return lax.cond(
            late,
            lambda left, final, *sources: right_products(left, gather(late_source(pairs, sources[0], final, times_dev))),
            lambda left, final, *sources: right_products(left, sources),
            left, terms[-1], *sources,
        )
    asked = asked_times(pairs, tm_size, pair_dev)
    first = first_time(pairs, tm_size, pair_dev, times_dev)
    slots = ready + [sum_of(terms[-1])]
    out = [pick(slots, slot_of(time, first, times_dev)) for time in asked]
    arrived = [
        shifted(jnp.stack(out[(d - 1) * pair_dev : d * pair_dev]), "tm", tm_size, d)
        for d in range(1, tm_size)
    ]
    sources = gather(choose_source(pairs, slots, arrived, tm_size, times_dev, pair_dev))
    return right_products(left, sources)


def late_source(pairs, source, final, times_dev):
    mine = pairs[lax.axis_index("tm"), 1] // times_dev == lax.axis_index("tm")
    return jnp.where(mine, sum_of(final)[None], source)


def solution(mesh):
    return jax.shard_map(
        local,
        mesh=mesh,
        in_specs=(
            P(("ens", "tm"), None, None, None, "space"),
            P("mom", None),
            P(),
            P(),
            P(("ens", "tm"), None, None, None, "space", None),
        ),
        out_specs=P(("ens", "tm"), "mom", None, "space", None),
        check_vma=False,
    )
```
